256 devices in a mesh: sample: 16 (over z, x_hi), seq: 16 (over y, x_lo, core).
Axes of the slice: x: 4 (x_hi: 2, x_lo: 2; x = x_hi * 2 + x_lo), y: 4, z: 8, core: 2. Of those that a mesh axis runs over, the one named last changes fastest.
Arguments:
- queries: bfloat16 [16, 2048, 8192], P('sample', 'seq'), may hold values from -900 to 900
- span_keys: bfloat16 [16, 2048, 1024], P('sample', 'seq'), may hold values from -6 to 6
- span_values: bfloat16 [16, 2048, 1024], P('sample', 'seq'), may hold values from -6 to 6
- prompt_keys: bfloat16 [2048, 1024], P('sample'), may hold values from -6 to 6
- prompt_values: bfloat16 [2048, 1024], P('sample'), may hold values from -6 to 6
- lengths: int32 [16], P('sample'), may hold values from 512 to 8192, as said below
- offsets: int32 [16], P('sample'), may hold values from 0 to 6144, as said below
Outputs:
- attended: bfloat16 [16, 2048, 8192], P('sample', 'seq')
The draws below stay inside these ranges and needn't reach their ends.
Inputs may be any that keep to these rules, and one draw needn't show every extreme that they name: A completion's block holds at least 512 live tokens: lengths[c] - offsets[c] >= 512. `offsets`: each offset is a whole multiple of 2048.
All inputs are finite; a program needn't handle non-finite values.
Results may differ from the reference program's by a relative error of at most 0.012.
The reference program's roundings to bfloat16 on the way count: a program that leaves them out, or rounds other values in their place, can miss the bound.
Values may be sent and summed in bfloat16 or wider, within the bound.
No kernel may reach another device: no remote copies, remote signals or barrier semaphores. Data moves between devices by JAX's collectives and lax.ppermute only.
A program may use at most 128 MiB of HBM per device.

```python
import math
import jax
import jax.numpy as jnp
from jax import lax

HEADS = 64
KV_HEADS = 8
HEAD_DIM = 128
SPAN = 2048
PROMPT = 2048
COMPLETIONS = 16


def block_plan(key):
    base_key = jax.random.fold_in(key, 7)
    index_key, extra_key = jax.random.split(base_key)
    span_index = jax.random.randint(index_key, (COMPLETIONS,), 0, 4)
    extra_rows = jax.random.randint(extra_key, (COMPLETIONS,), SPAN // 4, 2 * SPAN)
    numbers = jnp.arange(COMPLETIONS)
    span_index = jnp.where(numbers == 0, 3, jnp.where(numbers == 1, 0, span_index))
    offset_rows = span_index * SPAN
    length_rows = jnp.minimum(offset_rows + extra_rows, 4 * SPAN)
    length_rows = jnp.where(numbers == 0, 4 * SPAN, length_rows)
    return (length_rows.astype(jnp.int32), offset_rows.astype(jnp.int32))


def draw_lengths(key, part):
    return block_plan(key)[0]


def draw_offsets(key, part):
    return block_plan(key)[1]


def draw_queries(key, part):
    full_shape = (COMPLETIONS, SPAN, HEADS * HEAD_DIM)
    first_key = jax.random.fold_in(jax.random.fold_in(key, 11), 0)
    return (2.0 * jax.random.truncated_normal(first_key, -4.0, 4.0, full_shape, jnp.float32)).astype(jnp.bfloat16)


def level_of(rng, dims, shards, low, largest):
    loudness, own = 1.0, jax.random.fold_in(rng, 6)
    for position, parts in shards:
        heights = jnp.exp(jax.random.uniform(jax.random.fold_in(own, position), (parts,), jnp.float32, low / len(shards), largest / len(shards)))
        loudness = loudness * jnp.repeat(heights, dims[position] // parts).reshape([-1 if axis == position else 1 for axis in range(len(dims))])
    return loudness


def centred(own_key, shape, spread, limit, shards=(), kind=jnp.bfloat16):
    entries = jax.random.normal(own_key, shape, jnp.float32) * spread
    if len(shards) > 0:
        entries = level_of(own_key, shape, shards, -0.22, 0.18) * entries
    return jnp.clip(entries, min=-limit, max=limit).astype(kind)


def setup_inputs(seed: int = 0) -> dict:
    arg_keys = jax.random.split(jax.random.key(seed), 8)
    queries = draw_queries(jax.random.fold_in(arg_keys[7], 71), 0)
    span_keys = centred(arg_keys[1], (COMPLETIONS, SPAN, KV_HEADS * HEAD_DIM), 1.0, 6.0, ((0, 16), (1, 16)))
    span_values = centred(arg_keys[2], (COMPLETIONS, SPAN, KV_HEADS * HEAD_DIM), 1.0, 6.0, ((0, 16), (1, 16)))
    prompt_keys = centred(arg_keys[3], (PROMPT, KV_HEADS * HEAD_DIM), 1.0, 6.0, ((0, 16),))
    prompt_values = centred(arg_keys[4], (PROMPT, KV_HEADS * HEAD_DIM), 1.0, 6.0, ((0, 16),))
    lengths = draw_lengths(jax.random.fold_in(arg_keys[7], 71), 0)
    offsets = draw_offsets(jax.random.fold_in(arg_keys[7], 71), 0)
    return dict(queries=queries, span_keys=span_keys, span_values=span_values, prompt_keys=prompt_keys, prompt_values=prompt_values, lengths=lengths, offsets=offsets)


ROPE_BASE = 500000.0
NEG_FILL = -1e+30

def rope_angles(positions, head_size):
    half_dim = head_size // 2
    frequency = ROPE_BASE ** (-(jnp.arange(half_dim, dtype=jnp.float32) * (2.0 / head_size)))
    angles = positions.astype(jnp.float32)[:, None] * frequency[None, :]
    return (jnp.cos(angles), jnp.sin(angles))

def rotate(stacked, cos_table, sine_table):
    half_dim = stacked.shape[-1] // 2
    former = stacked[..., :half_dim]
    latter = stacked[..., half_dim:]
    cos_part = cos_table[:, None, :]
    sine_part = sine_table[:, None, :]
    return jnp.concatenate([former * cos_part - latter * sine_part, latter * cos_part + former * sine_part], axis=-1)

def reference(queries, span_keys, span_values, prompt_keys, prompt_values, lengths, offsets):
    group_size = HEADS // KV_HEADS
    scaling = 1.0 / math.sqrt(HEAD_DIM)
    prompt_kh = prompt_keys.reshape(PROMPT, KV_HEADS, HEAD_DIM)
    prompt_vh = prompt_values.reshape(PROMPT, KV_HEADS, HEAD_DIM)
    row_ids = jnp.arange(SPAN, dtype=jnp.int32)

    def completion(packed):
        query_rows, key_rows, value_rows, length, offset = packed
        positions = PROMPT + offset + row_ids
        cos_table, sine_table = rope_angles(positions, HEAD_DIM)
        rotated_q = rotate(query_rows.astype(jnp.float32).reshape(SPAN, HEADS, HEAD_DIM), cos_table, sine_table).astype(jnp.bfloat16)
        rotated_k = rotate(key_rows.astype(jnp.float32).reshape(SPAN, KV_HEADS, HEAD_DIM), cos_table, sine_table).astype(jnp.bfloat16)
        live_rows = offset + row_ids < length
        causal = (row_ids[None, :] <= row_ids[:, None]) & live_rows[None, :]
        allowed = jnp.concatenate([jnp.ones((SPAN, PROMPT), dtype=bool), causal], axis=1)
        all_keys = jnp.concatenate([prompt_kh, rotated_k], axis=0).transpose(1, 0, 2)
        all_values = jnp.concatenate([prompt_vh, value_rows.reshape(SPAN, KV_HEADS, HEAD_DIM)], axis=0).transpose(1, 0, 2)
        grouped = rotated_q.reshape(SPAN, KV_HEADS, group_size, HEAD_DIM).transpose(1, 0, 2, 3)

        def kv_head(inner):
            query_part, key_part, value_part = inner
            scores = jnp.einsum('qgd,kd->gqk', query_part.astype(jnp.float32), key_part.astype(jnp.float32)) * scaling
            scores = jnp.where(allowed[None], scores, NEG_FILL)
            row_top = lax.optimization_barrier(jnp.max(scores, axis=-1, keepdims=True))
            weights = jnp.exp(scores - row_top)
            totals = lax.optimization_barrier(jnp.sum(weights, axis=-1))
            rounded = lax.optimization_barrier(weights.astype(jnp.bfloat16)).astype(jnp.float32)
            mixture = jnp.einsum('gqk,kd->gqd', rounded, value_part.astype(jnp.float32))
            return mixture / totals[..., None]
        outputs = lax.map(kv_head, (grouped, all_keys, all_values))
        outputs = outputs.transpose(2, 0, 1, 3).reshape(SPAN, HEADS * HEAD_DIM)
        return jnp.where(live_rows[:, None], outputs, 0.0).astype(jnp.bfloat16)
    return lax.map(completion, (queries, span_keys, span_values, lengths, offsets))
```

```python
import math

import jax
import jax.numpy as jnp
from jax import lax
from jax.experimental import pallas as pl
from jax.experimental.pallas import tpu as pltpu
from jax.sharding import PartitionSpec as P


HEADS = 64
KV_HEADS = 8
HEAD_DIM = 128
ROPE_BASE = 500000.0
NEG_FILL = -1e30
GROUP = 16
CHIPS = 8
OWN = HEADS // GROUP
ROWS = 128
TILE = 512
WIDE = 1024
EXP_SCALE = math.log2(math.e) / math.sqrt(HEAD_DIM)


def rope_angles(positions, head_size):
    half_dim = head_size // 2
    frequency = ROPE_BASE ** (-(jnp.arange(half_dim, dtype=jnp.float32) * (2.0 / head_size)))
    angles = positions.astype(jnp.float32)[:, None] * frequency[None, :]
    return (jnp.cos(angles), jnp.sin(angles))


def turned(x, cos, sin):
    wide = x.astype(jnp.float32)
    return (wide * cos + pltpu.roll(wide, HEAD_DIM // 2, 1) * sin).astype(jnp.bfloat16)


def spread_body(info_ref, mine_ref, theirs_ref, cos_ref, sin_ref, keep_ref, give_ref):
    cos = cos_ref[...]
    sin = sin_ref[...]
    for head in range(OWN):
        columns = slice(head * HEAD_DIM, (head + 1) * HEAD_DIM)
        keep_ref[0, head] = turned(mine_ref[:, columns], cos, sin)
        give_ref[0, head] = turned(theirs_ref[:, columns], cos, sin)


def spread(info, queries, cos, sin):
    table = pl.BlockSpec((ROWS, HEAD_DIM), lambda d, info: (0, 0))
    piece = pl.BlockSpec((1, OWN, ROWS, HEAD_DIM), lambda d, info: (d, 0, 0, 0))
    shape = jax.ShapeDtypeStruct((CHIPS, OWN, ROWS, HEAD_DIM), jnp.bfloat16)
    return pl.pallas_call(
        spread_body,
        grid_spec=pltpu.PrefetchScalarGridSpec(
            num_scalar_prefetch=1,
            grid=(CHIPS,),
            in_specs=[
                pl.BlockSpec(
                    (ROWS, OWN * HEAD_DIM), lambda d, info: (0, (info[0] ^ d) * 2 + info[1])
                ),
                pl.BlockSpec(
                    (ROWS, OWN * HEAD_DIM), lambda d, info: (0, (info[0] ^ d) * 2 + (1 - info[1]))
                ),
                table,
                table,
            ],
            out_specs=[piece, piece],
        ),
        out_shape=[shape, shape],
        name="spread",
    )(info, queries, queries, cos, sin)


def spread_kv_body(key_ref, value_ref, cos_ref, sin_ref, out_ref):
    out_ref[0] = turned(key_ref[...], cos_ref[...], sin_ref[...])
    out_ref[1] = value_ref[...]


def spread_kv(keys, values, cos, sin):
    table = pl.BlockSpec((ROWS, HEAD_DIM), lambda h: (0, 0))
    head = pl.BlockSpec((ROWS, HEAD_DIM), lambda h: (0, h))
    return pl.pallas_call(
        spread_kv_body,
        grid=(KV_HEADS,),
        in_specs=[head, head, table, table],
        out_specs=pl.BlockSpec((2, ROWS, HEAD_DIM), lambda h: (h, 0, 0)),
        out_shape=jax.ShapeDtypeStruct((2 * KV_HEADS, ROWS, HEAD_DIM), jnp.bfloat16),
        name="spread_kv",
    )(keys, values, cos, sin)


def attend_body(info_ref, q_ref, kp_ref, vp_ref, ks_ref, vs_ref, before_ref, o_ref):
    chip = info_ref[0]
    core = info_ref[1]
    live = info_ref[2]
    prompt = kp_ref.shape[0]
    count = OWN * ROWS
    start = pl.multiple_of((chip // 2) * TILE, TILE)

    def half(which, unused):
        query = q_ref[which].reshape(count, HEAD_DIM)
        base = chip * (2 * ROWS) + (which ^ core) * ROWS

        def scores(keys):
            return lax.dot_general(
                query, keys, (((1,), (1,)), ((), ())), preferred_element_type=jnp.float32
            )

        def absorb(state, grids, values):
            new_top = jnp.max(grids, axis=1, keepdims=True)
            if state is not None:
                new_top = jnp.maximum(state[0], new_top)
            weights = jnp.exp2((grids - new_top) * EXP_SCALE)
            total = jnp.sum(weights, axis=1, keepdims=True)
            product = jnp.dot(
                weights.astype(jnp.bfloat16), values, preferred_element_type=jnp.float32
            )
            if state is not None:
                fade = jnp.exp2((state[0] - new_top) * EXP_SCALE)
                total = state[1] * fade + total
                product = state[2] * fade + product
            return new_top, total, product

        def places(width):
            index = lax.broadcasted_iota(jnp.int32, (OWN, ROWS, width), 1)
            return base + index.reshape(count, width)

        grids = scores(kp_ref[:WIDE, :])
        state = None
        for step in range(1, prompt // WIDE):
            ahead = scores(kp_ref[step * WIDE : (step + 1) * WIDE, :])
            state = absorb(state, grids, vp_ref[(step - 1) * WIDE : step * WIDE, :])
            grids = ahead
        ahead = scores(ks_ref[pl.ds(start, TILE), :])
        state = absorb(state, grids, vp_ref[prompt - WIDE :, :])
        column = start + lax.broadcasted_iota(jnp.int32, (count, TILE), 1)
        ahead = jnp.where(column <= places(TILE), ahead, NEG_FILL)
        state = absorb(state, ahead, vs_ref[pl.ds(start, TILE), :])

        def older(step, carried):
            begin = pl.multiple_of(step * TILE, TILE)
            return absorb(
                carried, scores(ks_ref[pl.ds(begin, TILE), :]), vs_ref[pl.ds(begin, TILE), :]
            )

        _, total, product = lax.fori_loop(0, chip // 2, older, state)
        outcome = jnp.where(places(HEAD_DIM) < live, product / total, 0.0)
        o_ref[which] = outcome.astype(jnp.bfloat16).reshape(OWN, ROWS, HEAD_DIM)
        return unused

    lax.fori_loop(0, 2, half, 0)


def attend(info, piece, kp, vp, ks, vs, before):
    whole = kp.shape[0] + ks.shape[0]
    pairs = 2 * OWN * ROWS * (kp.shape[0] + ks.shape[0] // 2)
    vmem = pl.BlockSpec(memory_space=pltpu.VMEM)
    return pl.pallas_call(
        attend_body,
        in_specs=[pl.BlockSpec(memory_space=pltpu.SMEM)]
        + [vmem] * 5
        + [pl.BlockSpec(memory_space=pl.ANY)],
        out_specs=vmem,
        out_shape=jax.ShapeDtypeStruct(piece.shape, jnp.bfloat16),
        compiler_params=pltpu.CompilerParams(vmem_limit_bytes=44 * 1024 * 1024),
        cost_estimate=pl.CostEstimate(
            flops=8 * pairs * HEAD_DIM, transcendentals=pairs, bytes_accessed=4 * whole * HEAD_DIM
        ),
        name="attend",
    )(info, piece, kp, vp, ks, vs, before)


def gather_body(info_ref, *refs):
    out_ref = refs[-1]
    twin_ref = refs[-2]
    for d in range(CHIPS):
        chip = info_ref[0] ^ d
        own = pl.multiple_of((chip * 2 + info_ref[1]) * (OWN * HEAD_DIM), HEAD_DIM)
        other = pl.multiple_of((chip * 2 + 1 - info_ref[1]) * (OWN * HEAD_DIM), HEAD_DIM)
        for head in range(OWN):
            out_ref[:, pl.ds(own + head * HEAD_DIM, HEAD_DIM)] = refs[d][0, head]
            out_ref[:, pl.ds(other + head * HEAD_DIM, HEAD_DIM)] = twin_ref[d, head]


def assemble(info, pieces, twin):
    vmem = pl.BlockSpec(memory_space=pltpu.VMEM)
    return pl.pallas_call(
        gather_body,
        in_specs=[pl.BlockSpec(memory_space=pltpu.SMEM)] + [vmem] * (CHIPS + 1),
        out_specs=vmem,
        out_shape=jax.ShapeDtypeStruct((ROWS, HEADS * HEAD_DIM), jnp.bfloat16),
        name="assemble",
    )(info, *pieces, twin)


def shards(queries, span_keys, span_values, prompt_keys, prompt_values, lengths, offsets):
    seq_index = lax.axis_index("seq")
    chip = seq_index // 2
    core = seq_index % 2
    local_rows = queries.shape[1]
    span = local_rows * GROUP
    prompt_local = prompt_keys.shape[0]
    prompt = prompt_local * lax.axis_size("sample")
    offset = offsets[0]
    live_count = jnp.clip(lengths[0] - offset, 0, span)
    info = jnp.stack([chip, core, live_count]).astype(jnp.int32)
    first_core = core == 0

    def twin_swap(x):
        return lax.ppermute(x, "seq", [(i, i ^ 1) for i in range(GROUP)])

    def chip_swap(x, d):
        return lax.ppermute(x, "seq", [(i, i ^ (2 * d)) for i in range(GROUP)])

    def key_and_value(mine):
        other = twin_swap(mine)
        return jnp.where(first_core, mine, other), jnp.where(first_core, other, mine)

    column = chip * HEAD_DIM
    picked = jnp.where(
        first_core,
        lax.dynamic_slice(prompt_keys, (0, column), (prompt_local, HEAD_DIM)),
        lax.dynamic_slice(prompt_values, (0, column), (prompt_local, HEAD_DIM)),
    )
    copies = jnp.broadcast_to(picked[None], (lax.axis_size("sample"), prompt_local, HEAD_DIM))
    prompt_mine = lax.all_to_all(copies, "sample", 0, 0, tiled=True).reshape(prompt, HEAD_DIM)
    kp, vp = key_and_value(prompt_mine)

    row_ids = seq_index * local_rows + jnp.arange(local_rows, dtype=jnp.int32)
    cos_table, sine_table = rope_angles(prompt + offset + row_ids, HEAD_DIM)
    cos_wide = jnp.concatenate([cos_table, cos_table], axis=1)
    sine_wide = jnp.concatenate([-sine_table, sine_table], axis=1)
    span_pieces = spread_kv(span_keys[0], span_values[0], cos_wide, sine_wide)
    span_mine = lax.all_to_all(span_pieces, "seq", 0, 0, tiled=True).reshape(span, HEAD_DIM)
    ks, vs = key_and_value(span_mine)

    keep, give = spread(info, queries[0], cos_wide, sine_wide)
    taken = twin_swap(give)
    sent = [jnp.stack([keep[d], taken[d]]) for d in range(CHIPS)]
    arrived = [sent[0]] + [chip_swap(sent[d], d) for d in range(1, CHIPS)]
    results = [None] * CHIPS
    done = arrived[1]
    for d in (*range(1, CHIPS), 0):
        place = jnp.stack([chip ^ d, core, live_count]).astype(jnp.int32)
        done = attend(place, arrived[d], kp, vp, ks, vs, done)
        results[d] = chip_swap(done, d) if d else done
    twin = twin_swap(jnp.stack([piece[1] for piece in results]))
    return assemble(info, results, twin)[None]


def solution(mesh):
    in_specs = (
        P("sample", "seq", None),
        P("sample", "seq", None),
        P("sample", "seq", None),
        P("sample", None),
        P("sample", None),
        P("sample"),
        P("sample"),
    )
    out_specs = P("sample", "seq", None)
    return jax.shard_map(shards, mesh=mesh, in_specs=in_specs, out_specs=out_specs, check_vma=False)
```

```python
import math

import jax
import jax.numpy as jnp
from jax import lax
from jax.experimental import pallas as pl
from jax.experimental.pallas import tpu as pltpu
from jax.sharding import PartitionSpec as P


HEADS = 64
KV_HEADS = 8
HEAD_DIM = 128
ROPE_BASE = 500000.0
NEG_FILL = -1e30
GROUP = 16
CHIPS = 8
OWN = HEADS // GROUP
ROWS = 128
BAND = 32
TILE = 512
WIDE = 1024
EXP_SCALE = math.log2(math.e) / math.sqrt(HEAD_DIM)


def rope_angles(positions, head_size):
    half_dim = head_size // 2
    frequency = ROPE_BASE ** (-(jnp.arange(half_dim, dtype=jnp.float32) * (2.0 / head_size)))
    angles = positions.astype(jnp.float32)[:, None] * frequency[None, :]
    return (jnp.cos(angles), jnp.sin(angles))


def turned(x, cos, sin):
    wide = x.astype(jnp.float32)
    return (wide * cos + pltpu.roll(wide, HEAD_DIM // 2, 1) * sin).astype(jnp.bfloat16)


def spread_body(info_ref, query_ref, cos_ref, sin_ref, keep_ref, give_ref):
    cos = cos_ref[...]
    sin = sin_ref[...]
    for d in range(CHIPS):
        own = ((info_ref[0] ^ d) * 2 + info_ref[1]) * (OWN * HEAD_DIM)
        other = ((info_ref[0] ^ d) * 2 + 1 - info_ref[1]) * (OWN * HEAD_DIM)
        for head in range(OWN):
            first = pl.multiple_of(own + head * HEAD_DIM, HEAD_DIM)
            second = pl.multiple_of(other + head * HEAD_DIM, HEAD_DIM)
            keep_ref[d, head] = turned(query_ref[:, pl.ds(first, HEAD_DIM)], cos, sin)
            give_ref[d, head] = turned(query_ref[:, pl.ds(second, HEAD_DIM)], cos, sin)


def spread(info, queries, cos, sin):
    table = pl.BlockSpec((BAND, HEAD_DIM), lambda r, info: (r, 0))
    piece = pl.BlockSpec((CHIPS, OWN, BAND, HEAD_DIM), lambda r, info: (0, 0, r, 0))
    shape = jax.ShapeDtypeStruct((CHIPS, OWN, ROWS, HEAD_DIM), jnp.bfloat16)
    return pl.pallas_call(
        spread_body,
        grid_spec=pltpu.PrefetchScalarGridSpec(
            num_scalar_prefetch=1,
            grid=(ROWS // BAND,),
            in_specs=[
                pl.BlockSpec((BAND, HEADS * HEAD_DIM), lambda r, info: (r, 0)),
                table,
                table,
            ],
            out_specs=[piece, piece],
        ),
        out_shape=[shape, shape],
        name="spread",
    )(info, queries, cos, sin)


def spread_kv_body(key_ref, value_ref, cos_ref, sin_ref, out_ref):
    cos = cos_ref[...]
    sin = sin_ref[...]
    for head in range(KV_HEADS):
        columns = slice(head * HEAD_DIM, (head + 1) * HEAD_DIM)
        out_ref[2 * head] = turned(key_ref[:, columns], cos, sin)
        out_ref[2 * head + 1] = value_ref[:, columns]


def spread_kv(keys, values, cos, sin):
    vmem = pl.BlockSpec(memory_space=pltpu.VMEM)
    return pl.pallas_call(
        spread_kv_body,
        in_specs=[vmem] * 4,
        out_specs=vmem,
        out_shape=jax.ShapeDtypeStruct((2 * KV_HEADS, ROWS, HEAD_DIM), jnp.bfloat16),
        name="spread_kv",
    )(keys, values, cos, sin)


def attend_body(info_ref, q_ref, kp_ref, vp_ref, ks_ref, vs_ref, before_ref, o_ref):
    chip = info_ref[0]
    core = info_ref[1]
    live = info_ref[2]
    prompt = kp_ref.shape[0]
    count = OWN * ROWS
    start = pl.multiple_of((chip // 2) * TILE, TILE)

    def half(which, unused):
        query = q_ref[which].reshape(count, HEAD_DIM)
        base = chip * (2 * ROWS) + (which ^ core) * ROWS

        def scores(keys):
            return lax.dot_general(
                query, keys, (((1,), (1,)), ((), ())), preferred_element_type=jnp.float32
            )

        def absorb(state, grids, values):
            new_top = jnp.max(grids, axis=1, keepdims=True)
            if state is not None:
                new_top = jnp.maximum(state[0], new_top)
            weights = jnp.exp2((grids - new_top) * EXP_SCALE)
            total = jnp.sum(weights, axis=1, keepdims=True)
            product = jnp.dot(
                weights.astype(jnp.bfloat16), values, preferred_element_type=jnp.float32
            )
            if state is not None:
                fade = jnp.exp2((state[0] - new_top) * EXP_SCALE)
                total = state[1] * fade + total
                product = state[2] * fade + product
            return new_top, total, product

        def places(width):
            index = lax.broadcasted_iota(jnp.int32, (OWN, ROWS, width), 1)
            return base + index.reshape(count, width)

        grids = scores(kp_ref[:WIDE, :])
        state = None
        for step in range(1, prompt // WIDE):
            ahead = scores(kp_ref[step * WIDE : (step + 1) * WIDE, :])
            state = absorb(state, grids, vp_ref[(step - 1) * WIDE : step * WIDE, :])
            grids = ahead
        ahead = scores(ks_ref[pl.ds(start, TILE), :])
        state = absorb(state, grids, vp_ref[prompt - WIDE :, :])
        column = start + lax.broadcasted_iota(jnp.int32, (count, TILE), 1)
        ahead = jnp.where(column <= places(TILE), ahead, NEG_FILL)
        state = absorb(state, ahead, vs_ref[pl.ds(start, TILE), :])

        def older(step, carried):
            begin = pl.multiple_of(step * TILE, TILE)
            return absorb(
                carried, scores(ks_ref[pl.ds(begin, TILE), :]), vs_ref[pl.ds(begin, TILE), :]
            )

        _, total, product = lax.fori_loop(0, chip // 2, older, state)
        outcome = jnp.where(places(HEAD_DIM) < live, product / total, 0.0)
        o_ref[which] = outcome.astype(jnp.bfloat16).reshape(OWN, ROWS, HEAD_DIM)
        return unused

    lax.fori_loop(0, 2, half, 0)


def attend(info, piece, kp, vp, ks, vs, before):
    whole = kp.shape[0] + ks.shape[0]
    pairs = 2 * OWN * ROWS * (kp.shape[0] + ks.shape[0] // 2)
    vmem = pl.BlockSpec(memory_space=pltpu.VMEM)
    return pl.pallas_call(
        attend_body,
        in_specs=[pl.BlockSpec(memory_space=pltpu.SMEM)]
        + [vmem] * 5
        + [pl.BlockSpec(memory_space=pl.ANY)],
        out_specs=vmem,
        out_shape=jax.ShapeDtypeStruct(piece.shape, jnp.bfloat16),
        compiler_params=pltpu.CompilerParams(vmem_limit_bytes=44 * 1024 * 1024),
        cost_estimate=pl.CostEstimate(
            flops=8 * pairs * HEAD_DIM, transcendentals=pairs, bytes_accessed=4 * whole * HEAD_DIM
        ),
        name="attend",
    )(info, piece, kp, vp, ks, vs, before)


def gather_body(info_ref, *refs):
    out_ref = refs[-1]
    twin_ref = refs[-2]
    for d in range(CHIPS):
        chip = info_ref[0] ^ d
        own = (chip * 2 + info_ref[1]) * (OWN * HEAD_DIM)
        other = (chip * 2 + 1 - info_ref[1]) * (OWN * HEAD_DIM)
        for head in range(OWN):
            first = pl.multiple_of(own + head * HEAD_DIM, HEAD_DIM)
            second = pl.multiple_of(other + head * HEAD_DIM, HEAD_DIM)
            out_ref[:, pl.ds(first, HEAD_DIM)] = refs[d][0, head]
            out_ref[:, pl.ds(second, HEAD_DIM)] = twin_ref[d, head]


def assemble(info, pieces, twin):
    half = pl.BlockSpec((1, OWN, BAND, HEAD_DIM), lambda r, info: (0, 0, r, 0))
    return pl.pallas_call(
        gather_body,
        grid_spec=pltpu.PrefetchScalarGridSpec(
            num_scalar_prefetch=1,
            grid=(ROWS // BAND,),
            in_specs=[half] * CHIPS
            + [pl.BlockSpec((CHIPS, OWN, BAND, HEAD_DIM), lambda r, info: (0, 0, r, 0))],
            out_specs=pl.BlockSpec((BAND, HEADS * HEAD_DIM), lambda r, info: (r, 0)),
        ),
        out_shape=jax.ShapeDtypeStruct((ROWS, HEADS * HEAD_DIM), jnp.bfloat16),
        name="assemble",
    )(info, *pieces, twin)


def scored(queries, span_keys, span_values, prompt_keys, prompt_values, lengths, offsets):
    seq_index = lax.axis_index("seq")
    chip = seq_index // 2
    core = seq_index % 2
    local_rows = queries.shape[1]
    span = local_rows * GROUP
    prompt_local = prompt_keys.shape[0]
    prompt = prompt_local * lax.axis_size("sample")
    offset = offsets[0]
    live_count = jnp.clip(lengths[0] - offset, 0, span)
    info = jnp.stack([chip, core, live_count]).astype(jnp.int32)
    first_core = core == 0

    def twin_swap(x):
        return lax.ppermute(x, "seq", [(i, i ^ 1) for i in range(GROUP)])

    def chip_swap(x, d):
        return lax.ppermute(x, "seq", [(i, i ^ (2 * d)) for i in range(GROUP)])

    def key_and_value(mine):
        other = twin_swap(mine)
        return jnp.where(first_core, mine, other), jnp.where(first_core, other, mine)

    column = chip * HEAD_DIM
    picked = jnp.where(
        first_core,
        lax.dynamic_slice(prompt_keys, (0, column), (prompt_local, HEAD_DIM)),
        lax.dynamic_slice(prompt_values, (0, column), (prompt_local, HEAD_DIM)),
    )
    copies = jnp.broadcast_to(picked[None], (lax.axis_size("sample"), prompt_local, HEAD_DIM))
    prompt_mine = lax.all_to_all(copies, "sample", 0, 0, tiled=True)
    prompt_mine = prompt_mine.reshape(prompt, HEAD_DIM)
    kp, vp = key_and_value(prompt_mine)

    row_ids = seq_index * local_rows + jnp.arange(local_rows, dtype=jnp.int32)
    cos_table, sine_table = rope_angles(prompt + offset + row_ids, HEAD_DIM)
    cos_wide = jnp.concatenate([cos_table, cos_table], axis=1)
    sine_wide = jnp.concatenate([-sine_table, sine_table], axis=1)
    span_pieces = spread_kv(span_keys[0], span_values[0], cos_wide, sine_wide)
    span_mine = lax.all_to_all(span_pieces, "seq", 0, 0, tiled=True)
    span_mine = span_mine.reshape(span, HEAD_DIM)
    ks, vs = key_and_value(span_mine)

    keep, give = spread(info, queries[0], cos_wide, sine_wide)
    taken = twin_swap(give)
    sent = [jnp.stack([keep[d], taken[d]]) for d in range(CHIPS)]
    arrived = [sent[0]] + [chip_swap(sent[d], d) for d in range(1, CHIPS)]
    results = [None] * CHIPS
    done = arrived[1]
    for d in (*range(1, CHIPS), 0):
        place = jnp.stack([chip ^ d, core, live_count]).astype(jnp.int32)
        done = attend(place, arrived[d], kp, vp, ks, vs, done)
        results[d] = chip_swap(done, d) if d else done
    twin = twin_swap(jnp.stack([piece[1] for piece in results]))
    return assemble(info, results, twin)[None]


def solution(mesh):
    in_specs = (
        P("sample", "seq", None),
        P("sample", "seq", None),
        P("sample", "seq", None),
        P("sample", None),
        P("sample", None),
        P("sample"),
        P("sample"),
    )
    out_specs = P("sample", "seq", None)
    return jax.shard_map(scored, mesh=mesh, in_specs=in_specs, out_specs=out_specs, check_vma=False)
```
